256 devices in a mesh: expert: 64 (over x, z, core), tensor: 4 (over y).
Axes of the slice: x: 4, y: 4, z: 8, core: 2. Of those that a mesh axis runs over, the one named last changes fastest.
Arguments:
- tokens: bfloat16 [4096, 7168], P('expert', 'tensor'), may hold values from -48 to 48
- expert_ids: int32 [4096, 8], P('expert'), may hold values from 0 to 63, all different within a row; in each aligned block of 64 rows (0 to 63, 64 to 127, ...) at most 12 rows name the same one
- route_weights: float32 [4096, 8], P('expert'), may hold values from 0.02 to 0.2
- gate_weight: bfloat16 [64, 7168, 1024], P('expert', None, 'tensor'), may hold values from -0.0625 to 0.0625
- up_weight: bfloat16 [64, 7168, 1024], P('expert', None, 'tensor'), may hold values from -0.0625 to 0.0625
- down_weight: bfloat16 [64, 1024, 7168], P('expert', 'tensor'), may hold values from -0.1875 to 0.1875
Outputs:
- layer_out: bfloat16 [4096, 7168], P('expert', 'tensor')
- scales: float32 [7168], P('tensor')
The draws below stay inside these ranges and needn't reach their ends.
Inputs may be any that keep to these rules, and one draw needn't show every extreme that they name: `expert_ids`: each row names 8 different experts. Among the 64 rows of one index of expert (aligned blocks of rows) no expert is named by more than 12 rows, and in every draw some expert is named by exactly 12 rows of some block.
All inputs are finite; a program needn't handle non-finite values.
Results may differ from the reference program's by a relative error of at most 0.015.
Values may be sent and summed in bfloat16 or wider, within the bound.
A program may use at most 128 MiB of HBM per device.

```python
import math
import jax
import jax.numpy as jnp
import numpy as np
from jax import lax

D = 7168
FF = 1024
TOP = 8
TOK_DEV = 64
EXPERTS = 64
TOKENS = 4096
CAP = 12
HID_DEV = 256
N_TENSOR = 4


def draw_tokens(key, part):
    noise_key, channel_key, row_key = jax.random.split(jax.random.fold_in(key, 11), 3)
    channel = jnp.exp(jax.random.uniform(channel_key, (1, D), jnp.float32, 0.0, math.log(10.0)))
    rising = 1.0 + 2.0 * jnp.arange(TOKENS, dtype=jnp.float32)[:, None] / max(TOKENS - 1, 1)
    row_scale = rising * jnp.exp(jax.random.uniform(row_key, (TOKENS, 1), jnp.float32, 0.0, math.log(4.0)))
    noise = jnp.clip(jax.random.normal(noise_key, (TOKENS, D), jnp.float32), -4.0, 4.0)
    return jnp.clip(0.12 * noise * channel * row_scale, -48.0, 48.0).astype(jnp.bfloat16)


def level_of(key, dims, cuts, smallest, largest):
    gain = 1.0
    for dim, parts in cuts:
        heights = jax.random.uniform(jax.random.fold_in(jax.random.fold_in(key, 6), dim), (parts,), jnp.float32, smallest / len(cuts), largest / len(cuts))
        gain = gain * jnp.repeat(jnp.exp(heights), dims[dim] // parts).reshape((-1,) + (1,) * (len(dims) - 1 - dim))
    return gain


def routed_block(stream_key, own, number, rows, count, top, most, lean):
    ranking = jax.random.permutation(stream_key, count)
    heavy_load, usual = portions_of(count, rows * top, most, lean, True), portions_of(count, rows * top, most, lean, False)
    places = jnp.arange(count)

    def named(tallies, offset_by):
        used = int((tallies > 0).sum())
        fixed = max(1, used // 4)
        passed = fixed + (places - fixed + offset_by * (used - fixed)) % max(1, count - fixed)
        return jnp.zeros((count,), jnp.int32).at[ranking[jnp.where(places < fixed, places, passed)]].set(jnp.asarray(tallies, jnp.int32))

    tallies = jnp.where(number % 4 == 0, named(heavy_load, number // 4), named(usual, number - number // 4 - 1))
    mixed = jax.random.permutation(jax.random.fold_in(own, 3), count)
    source_of, taker = mixed[0:count // 2 * 2:2], mixed[1:count // 2 * 2:2]
    room = jnp.minimum(tallies[source_of] - 1, most - tallies[taker]) // 2
    room = jnp.where((source_of == ranking[0]) | (taker == ranking[0]) | (tallies[taker] == 0), 0, jnp.maximum(room, 0))
    passed = jax.random.randint(jax.random.fold_in(own, 4), (count // 2,), 0, 1 << 20) % (room + 1)
    tallies = tallies.at[source_of].add(-passed).at[taker].add(passed)
    members = jnp.searchsorted(jnp.cumsum(tallies), jnp.arange(rows * top), side="right").astype(jnp.int32)
    listing = members.reshape(top, rows).T
    listing = listing[jax.random.permutation(jax.random.fold_in(own, 1), rows)]
    offset_by = jax.random.randint(jax.random.fold_in(own, 2), (rows, 1), 0, top)
    return jnp.take_along_axis(listing, (jnp.arange(top)[None, :] + offset_by) % top, axis=1)


def portions_of(number_of, total, most, slope, full):
    loads = [(1 << 20) // math.isqrt(rank ** slope) + 1 for rank in range(1, number_of + 1)]
    largest = most if full else min(most, max(-(-total // number_of), total * loads[0] // sum(loads)))
    least = 1 if total - largest >= number_of - 1 else 0
    counts, surplus = [largest] + [least] * (number_of - 1), total - largest - least * (number_of - 1)
    while surplus > 0:
        movable = [i for i in range(1, number_of) if counts[i] < largest] or [i for i in range(1, number_of) if counts[i] < most]
        mass, left = sum([loads[i] for i in movable]), surplus
        for i in movable:
            more = min(most - counts[i], max(1, left * loads[i] // mass), surplus)
            counts[i] = counts[i] + more
            surplus = surplus - more
    return np.array(counts)


def gaussian(key, shape, deviation, most, cuts=(), held_as=jnp.bfloat16):
    level = level_of(key, shape, cuts, -0.22, 0.18) if cuts else 1.0
    result = jax.random.normal(key, shape, jnp.float32) * deviation * level
    return jnp.minimum(jnp.maximum(result, -most), most).astype(held_as)


def setup_inputs(seed: int = 0) -> dict:
    splits = jax.random.split(jax.random.key(seed), 7)
    tokens = draw_tokens(jax.random.fold_in(splits[6], 71), 0)
    expert_ids_keys = jax.random.split(jax.random.fold_in(splits[1], 1), TOKENS // TOK_DEV)
    expert_ids_turns = jax.random.permutation(jax.random.fold_in(splits[1], 3), TOKENS // TOK_DEV)
    expert_ids = jax.vmap(lambda own, number: routed_block(jax.random.fold_in(splits[1], 2), own, number, TOK_DEV, EXPERTS, TOP, CAP, 2))(expert_ids_keys, expert_ids_turns).reshape((TOKENS, TOP))
    route_weights = jnp.clip(0.02 + 0.18 * jax.random.uniform(splits[2], (TOKENS, TOP), jnp.float32) ** level_of(splits[2], (TOKENS, TOP), ((0, 64),), -0.2, 0.2), 0.02, 0.2)
    gate_weight = gaussian(splits[3], (EXPERTS, D, FF), D ** -0.5, 0.0625, ((0, 64), (2, 4)))
    up_weight = gaussian(splits[4], (EXPERTS, D, FF), D ** -0.5, 0.0625, ((0, 64), (2, 4)))
    down_weight = gaussian(splits[5], (EXPERTS, FF, D), FF ** -0.5, 0.1875, ((0, 64), (1, 4)))
    return {"tokens": tokens, "expert_ids": expert_ids, "route_weights": route_weights, "gate_weight": gate_weight, "up_weight": up_weight, "down_weight": down_weight}


EPS = 1e-05
CLIP_SHARE = 0.5

def channel_max(weights_pair):
    gate_rows, up_rows = weights_pair
    return jnp.maximum(lax.optimization_barrier(jnp.max(jnp.abs(gate_rows), axis=1)), lax.optimization_barrier(jnp.max(jnp.abs(up_rows), axis=1))).astype(jnp.float32)

def reference(tokens, expert_ids, route_weights, gate_weight, up_weight, down_weight):
    capacity_rows = EXPERTS * CAP
    act_max = lax.optimization_barrier(jnp.max(jnp.abs(tokens), axis=0)).astype(jnp.float32)
    wt_max = lax.optimization_barrier(jnp.max(lax.map(channel_max, (gate_weight, up_weight)), axis=0))
    scales = jnp.sqrt((act_max + EPS) / (wt_max + EPS))
    clip_limit = CLIP_SHARE * jnp.max(act_max / scales)
    smoothed = jnp.clip(tokens.astype(jnp.float32) / scales, -clip_limit, clip_limit).astype(jnp.bfloat16)
    token_numbers = jnp.arange(TOKENS, dtype=jnp.int32)

    def per_expert(accumulated, expert):
        chosen = expert_ids == expert
        weight = lax.optimization_barrier(jnp.sum(jnp.where(chosen, route_weights, jnp.float32(0.0)), axis=1))
        present = jnp.any(chosen, axis=1)
        position = jnp.cumsum(present.astype(jnp.int32)) - 1
        target = jnp.where(present, position, capacity_rows).astype(jnp.int32)
        row_index = jnp.zeros((capacity_rows,), jnp.int32).at[target].set(token_numbers, mode='drop')
        filled = jnp.zeros((capacity_rows,), jnp.bool_).at[target].set(True, mode='drop')
        picked = smoothed[row_index]
        gate_folded = (scales[:, None] * gate_weight[expert].astype(jnp.float32)).astype(jnp.bfloat16)
        up_folded = (scales[:, None] * up_weight[expert].astype(jnp.float32)).astype(jnp.bfloat16)
        gate_act = jnp.dot(picked, gate_folded, preferred_element_type=jnp.float32)
        up_act = jnp.dot(picked, up_folded, preferred_element_type=jnp.float32)
        hidden = (jax.nn.silu(gate_act) * up_act).astype(jnp.bfloat16)
        pieces = hidden.reshape(capacity_rows, N_TENSOR, HID_DEV).astype(jnp.float32)
        down_pieces = down_weight[expert].reshape(N_TENSOR, HID_DEV, D).astype(jnp.float32)
        partial_value = jnp.einsum('rgh,ghd->grd', pieces, down_pieces).astype(jnp.bfloat16)
        expert_out = lax.optimization_barrier(jnp.sum(partial_value.astype(jnp.float32), axis=0)).astype(jnp.bfloat16)
        weighted = jnp.where(filled, weight[row_index], jnp.float32(0.0))[:, None] * expert_out.astype(jnp.float32)
        return (accumulated.at[row_index].add(weighted), None)
    start_sum = jnp.zeros((TOKENS, D), jnp.float32)
    accumulated, unused = lax.scan(per_expert, start_sum, jnp.arange(EXPERTS, dtype=jnp.int32))
    return (accumulated.astype(jnp.bfloat16), scales)
```

```python
import functools

import jax
import jax.numpy as jnp
import numpy as np
from jax import lax
from jax.experimental import pallas as pl
from jax.experimental.pallas import tpu as pltpu
from jax.sharding import PartitionSpec as P

EPS = 1e-05
CLIP_SHARE = 0.5
MESH = pl.DeviceIdType.MESH

NX, NZ, NC = 4, 8, 2
NG = NX * NC
NY = 4
CAP = 12
TOK = 64
TOP = 8
WIDTH = 1792
D = NY * WIDTH
HID = 256
PIECE = NZ * CAP
ROWS = NG * PIECE
STOK = NZ * TOK
CODE = 16
AUX = 128
WROWS = D // 128
AROWS = WIDTH // 128
MROWS = -(-(WROWS + AROWS) // 8) * 8
RIGHT, LEFT = NZ // 2, NZ - 1 - NZ // 2
COLT = 256
HALF = ROWS // 2


def place():
    me = lax.axis_index("expert")
    x = me // (NZ * NC)
    z = lax.rem(me // NC, NZ)
    c = lax.rem(me, NC)
    return x, z, c, lax.axis_index("tensor")


def expert_at(group, z):
    return (group // NC) * (NZ * NC) + z * NC + lax.rem(group, NC)


def enter(peers):
    barrier = pltpu.get_barrier_semaphore()
    for peer in peers:
        pl.semaphore_signal(barrier, inc=1, device_id=peer, device_id_type=MESH)
    pl.semaphore_wait(barrier, len(peers))


def neighbours():
    x, z, c, y = place()
    g = x * NC + c
    up = (expert_at(g, lax.rem(z + 1, NZ)), y)
    down = (expert_at(g, lax.rem(z + NZ - 1, NZ)), y)
    group = [(expert_at(lax.rem(g + j, NG), z), y) for j in range(1, NG)]
    me = expert_at(g, z)
    column = [(me, lax.rem(y + j, NY)) for j in range(1, NY)]
    return z, g, y, up, down, group, column


def remote(src, dst, send, recv, peer):
    return pltpu.make_async_remote_copy(
        src_ref=src, dst_ref=dst, send_sem=send, recv_sem=recv, device_id=peer, device_id_type=MESH
    )


def dispatch_kernel(
    tok_ref, aux_ref, keyrow_ref, keycol_ref, down_ref,
    rows_ref, dn_ref, comb_ref, most_ref,
    tbuf, abuf, pick, sendbuf, mx, my_ref,
    d_send, d_recv, tr_send, tr_recv, tl_send, tl_recv,
    ar_send, ar_recv, al_send, al_recv,
    x_send, x_recv, m_send, m_recv, y_send, y_recv, loc_sem,
):
    z, g, y, up, down, group, column = neighbours()
    enter([up, down] + group + column)

    own_tok = pltpu.make_async_copy(tok_ref, tbuf.at[z], loc_sem.at[0])
    own_aux = pltpu.make_async_copy(aux_ref, abuf.at[z], loc_sem.at[1])
    own_tok.start()
    own_aux.start()

    def ring(own, buf, send, recv, peer, step, way):
        slot = lax.rem(z - way * step + NZ, NZ)
        src = own if step == 0 else buf.at[slot]
        return remote(src, buf.at[slot], send.at[step], recv.at[step], peer)

    tr = [ring(tok_ref, tbuf, tr_send, tr_recv, up, i, 1) for i in range(RIGHT)]
    tl = [ring(tok_ref, tbuf, tl_send, tl_recv, down, i, -1) for i in range(LEFT)]
    ar = [ring(aux_ref, abuf, ar_send, ar_recv, up, i, 1) for i in range(RIGHT)]
    al = [ring(aux_ref, abuf, al_send, al_recv, down, i, -1) for i in range(LEFT)]
    ar[0].start()
    al[0].start()
    tr[0].start()
    tl[0].start()

    own_down = pltpu.make_async_copy(
        down_ref.at[:, pl.ds(pl.multiple_of(y * WIDTH, 128), WIDTH)], dn_ref.at[y], loc_sem.at[2]
    )
    own_down.start()
    dcopies = []
    for j in range(1, NY):
        to = lax.rem(y + j, NY)
        dcopies.append(
            remote(
                down_ref.at[:, pl.ds(pl.multiple_of(to * WIDTH, 128), WIDTH)],
                dn_ref.at[y], d_send.at[j - 1], d_recv.at[j - 1], column[j - 1],
            )
        )
    for copy in dcopies:
        copy.start()

    for i in range(RIGHT):
        ar[i].wait_recv()
        if i + 1 < RIGHT:
            ar[i + 1].start()
        if i < LEFT:
            al[i].wait_recv()
            if i + 1 < LEFT:
                al[i + 1].start()
    own_aux.wait()
    tr[0].wait_recv()
    tr[1].start()
    tl[0].wait_recv()
    if LEFT > 1:
        tl[1].start()

    @pl.loop(0, NZ)
    def _(b):
        block = abuf[b, 0:TOK, :].astype(jnp.float32)
        total = jnp.zeros((TOK, ROWS), jnp.float32)
        for k in range(TOP):
            code = block[:, k : k + 1] * CODE + block[:, TOP + k : TOP + k + 1] + (b * 1024).astype(jnp.float32)
            weight = block[:, 2 * TOP + k : 2 * TOP + k + 1]
            total = total + jnp.where(code == keyrow_ref[0:1, :], weight, 0.0)
        comb_ref[pl.ds(pl.multiple_of(b * TOK, TOK), TOK), :] = total.astype(jnp.bfloat16)

    for i in range(1, RIGHT - 1):
        tr[i].wait_recv()
        tr[i + 1].start()
        if i < LEFT:
            tl[i].wait_recv()
            if i + 1 < LEFT:
                tl[i + 1].start()

    codes = []
    for b in range(NZ):
        block = abuf[b, 0:TOK, :].astype(jnp.float32)
        code = block * CODE + pltpu.roll(block, AUX - TOP, 1) + float(b * 1024)
        codes.append(code)
    code_t = jnp.transpose(jnp.concatenate(codes, axis=0))

    for r in range(0, ROWS, 96):
        key = keycol_ref[r : r + 96, 0:1]
        hit = key == code_t[0:1, :]
        for k in range(1, TOP):
            hit = hit | (key == code_t[k : k + 1, :])
        pick[r : r + 96, :] = jnp.where(hit, 1.0, 0.0).astype(jnp.bfloat16)

    wt = abuf[0, TOK : TOK + WROWS, :].astype(jnp.float32)
    for b in range(1, NZ):
        wt = jnp.maximum(wt, abuf[b, TOK : TOK + WROWS, :].astype(jnp.float32))
    mx[g] = jnp.zeros((MROWS, 128), jnp.float32)
    mx[g, 0:WROWS, :] = wt

    tr[RIGHT - 1].wait_recv()
    own_tok.wait()

    for n in range(0, WIDTH, COLT):
        tile = tbuf[:, :, n : n + COLT].reshape(STOK, COLT)
        got = jnp.dot(pick[...], tile, preferred_element_type=jnp.float32)
        sendbuf[:, :, n : n + COLT] = got.astype(jnp.bfloat16).reshape(NG, PIECE, COLT)
        top = jnp.max(jnp.abs(tile.astype(jnp.float32)), axis=0, keepdims=True)
        for q in range(COLT // 128):
            mx[g, WROWS + n // 128 + q : WROWS + n // 128 + q + 1, :] = top[:, q * 128 : q * 128 + 128]

    mcopies = [
        remote(mx.at[g], mx.at[g], m_send.at[j], m_recv.at[j], group[j]) for j in range(NG - 1)
    ]
    xcopies = [
        remote(sendbuf.at[lax.rem(g + j + 1, NG)], rows_ref.at[g], x_send.at[j], x_recv.at[j], group[j])
        for j in range(NG - 1)
    ]
    own_rows = pltpu.make_async_copy(sendbuf.at[g], rows_ref.at[g], loc_sem.at[3])
    for copy in mcopies:
        copy.start()
    for copy in xcopies:
        copy.start()
    own_rows.start()
    for copy in mcopies:
        copy.wait_recv()
    most = mx[0]
    for j in range(1, NG):
        most = jnp.maximum(most, mx[j])
    my_ref[y] = most
    ycopies = [
        remote(my_ref.at[y], my_ref.at[y], y_send.at[j], y_recv.at[j], column[j]) for j in range(NY - 1)
    ]
    for copy in ycopies:
        copy.start()
    for copy in ycopies + dcopies:
        copy.wait()
    most_ref[...] = my_ref[...]
    for copy in xcopies:
        copy.wait()
    for copy in mcopies + tr + tl + ar + al:
        copy.wait_send()
    own_rows.wait()
    own_down.wait()


def dispatch(tokens, aux, keyrow, keycol, down_local):
    vmem = pl.BlockSpec(memory_space=pltpu.VMEM)
    anyspace = pl.BlockSpec(memory_space=pl.ANY)
    dma = pltpu.SemaphoreType.DMA
    bf, f32 = jnp.bfloat16, jnp.float32
    return pl.pallas_call(
        dispatch_kernel,
        out_shape=(
            jax.ShapeDtypeStruct((NG, PIECE, WIDTH), bf),
            jax.ShapeDtypeStruct((NY, HID, WIDTH), bf),
            jax.ShapeDtypeStruct((STOK, ROWS), bf),
            jax.ShapeDtypeStruct((NY, MROWS, 128), f32),
        ),
        in_specs=[vmem, vmem, vmem, vmem, anyspace],
        out_specs=(anyspace, anyspace, vmem, vmem),
        scratch_shapes=[
            pltpu.VMEM((NZ, TOK, WIDTH), bf),
            pltpu.VMEM((NZ, AUX, 128), bf),
            pltpu.VMEM((ROWS, STOK), bf),
            pltpu.VMEM((NG, PIECE, WIDTH), bf),
            pltpu.VMEM((NG, MROWS, 128), f32),
            pltpu.VMEM((NY, MROWS, 128), f32),
            dma((NY - 1,)), dma((NY - 1,)),
            dma((RIGHT,)), dma((RIGHT,)), dma((LEFT,)), dma((LEFT,)),
            dma((RIGHT,)), dma((RIGHT,)), dma((LEFT,)), dma((LEFT,)),
            dma((NG - 1,)), dma((NG - 1,)), dma((NG - 1,)), dma((NG - 1,)),
            dma((NY - 1,)), dma((NY - 1,)), dma((4,)),
        ],
        compiler_params=pltpu.CompilerParams(
            collective_id=0, has_side_effects=True, vmem_limit_bytes=60 * 1024 * 1024
        ),
        name="dispatch",
    )(tokens, aux, keyrow, keycol, down_local)


def expert_kernel(
    rows_ref, gate_ref, up_ref, thr_ref, dn_ref, comb_ref,
    out_ref,
    xbuf, wg, wu, accg, accu, hbuf, dn, obuf, rbuf, part, rsend, rrecv, lsend, lrecv,
    yr_send, yr_recv, yl_send, yl_recv,
    hr_send, hr_recv, hl_send, hl_recv,
    x_send, x_recv, zr_send, zr_recv, zl_send, zl_recv, loc_sem,
):
    z, g, y, up, down, group, column = neighbours()
    nxt, prv = column[0], column[NY - 2]
    enter([up, down] + group + column)
    lo, hi = pl.ds(0, HALF), pl.ds(HALF, HALF)

    yr = [
        remote(rows_ref.at[lo], xbuf.at[1, lo], yr_send.at[0], yr_recv.at[0], nxt),
        remote(rows_ref.at[hi], xbuf.at[1, hi], yr_send.at[1], yr_recv.at[1], nxt),
        remote(xbuf.at[1, lo], xbuf.at[3, lo], yr_send.at[2], yr_recv.at[2], nxt),
    ]
    yl = [
        remote(rows_ref.at[hi], xbuf.at[2, hi], yl_send.at[0], yl_recv.at[0], prv),
        remote(rows_ref.at[lo], xbuf.at[2, lo], yl_send.at[1], yl_recv.at[1], prv),
        remote(xbuf.at[2, hi], xbuf.at[3, hi], yl_send.at[2], yl_recv.at[2], prv),
    ]
    for i in range(2):
        yr[i].start()
        yl[i].start()
    loads = [
        pltpu.make_async_copy(rows_ref, xbuf.at[0], loc_sem.at[0]),
        pltpu.make_async_copy(gate_ref, wg, loc_sem.at[1]),
        pltpu.make_async_copy(up_ref, wu, loc_sem.at[2]),
        pltpu.make_async_copy(dn_ref, dn, loc_sem.at[3]),
    ]
    for copy in loads:
        copy.start()
    for copy in loads:
        copy.wait()

    def add(slot, owner, start, count, first):
        krows = pl.ds(pl.multiple_of(owner * WIDTH, 256), WIDTH)
        bound = thr_ref[pl.ds(pl.multiple_of(owner * 16, 16), 16), :][0:1, :]

        @pl.loop(0, count // HALF)
        def _(i):
            sl = pl.ds(pl.multiple_of(start + i * HALF, HALF), HALF)
            x = jnp.minimum(jnp.maximum(xbuf[slot, sl, :], -bound), bound)
            a = jnp.dot(x, wg[krows, :], preferred_element_type=jnp.float32)
            b = jnp.dot(x, wu[krows, :], preferred_element_type=jnp.float32)
            if first:
                accg[sl, :] = a
                accu[sl, :] = b
            else:
                accg[sl, :] += a
                accu[sl, :] += b

    left, right, far = lax.rem(y + NY - 1, NY), lax.rem(y + 1, NY), lax.rem(y + 2, NY)
    add(0, y, 0, ROWS, True)
    yr[0].wait_recv()
    yr[2].start()
    yl[0].wait_recv()
    yl[2].start()
    add(1, left, 0, HALF, False)
    add(2, right, HALF, HALF, False)
    yr[1].wait_recv()
    add(1, left, HALF, HALF, False)
    yl[1].wait_recv()
    add(2, right, 0, HALF, False)

    def hidden(sl):
        v = accg[sl, :]
        hbuf[y, sl, :] = (v / (1.0 + jnp.exp(-v)) * accu[sl, :]).astype(jnp.bfloat16)

    hr = [
        remote(hbuf.at[y, lo], hbuf.at[y, lo], hr_send.at[0], hr_recv.at[0], nxt),
        remote(hbuf.at[y, hi], hbuf.at[y, hi], hr_send.at[1], hr_recv.at[1], nxt),
        remote(hbuf.at[left, lo], hbuf.at[left, lo], hr_send.at[2], hr_recv.at[2], nxt),
    ]
    hl = [
        remote(hbuf.at[y, lo], hbuf.at[y, lo], hl_send.at[0], hl_recv.at[0], prv),
        remote(hbuf.at[y, hi], hbuf.at[y, hi], hl_send.at[1], hl_recv.at[1], prv),
        remote(hbuf.at[right, hi], hbuf.at[right, hi], hl_send.at[2], hl_recv.at[2], prv),
    ]
    yr[2].wait_recv()
    add(3, far, 0, HALF, False)
    hidden(lo)
    hr[0].start()
    hl[0].start()
    yl[2].wait_recv()
    add(3, far, HALF, HALF, False)
    hidden(hi)
    hr[1].start()
    hl[1].start()
    hr[0].wait_recv()
    hr[2].start()
    hl[0].wait_recv()
    hl[1].wait_recv()
    hl[2].start()
    hr[1].wait_recv()
    hr[2].wait_recv()
    hl[2].wait_recv()

    @pl.loop(0, WIDTH // COLT)
    def _(i):
        cols = pl.ds(pl.multiple_of(i * COLT, COLT), COLT)
        acc = jnp.dot(hbuf[0], dn[0:HID, cols], preferred_element_type=jnp.float32)
        for q in range(1, NY):
            acc += jnp.dot(
                hbuf[q], dn[q * HID : (q + 1) * HID, cols], preferred_element_type=jnp.float32
            )
        obuf[:, cols] = acc.astype(jnp.bfloat16)

    def piece(j):
        return pl.ds(pl.multiple_of(j * PIECE, PIECE), PIECE)

    xcopies = [
        remote(obuf.at[piece(lax.rem(g + j + 1, NG))], rbuf.at[piece(g)], x_send.at[j], x_recv.at[j], group[j])
        for j in range(NG - 1)
    ]
    own = pltpu.make_async_copy(obuf.at[piece(g)], rbuf.at[piece(g)], loc_sem.at[4])
    for copy in xcopies:
        copy.start()
    own.start()
    for copy in xcopies:
        copy.wait_recv()
    own.wait()

    @pl.loop(0, WIDTH // COLT)
    def _(i):
        cols = pl.ds(pl.multiple_of(i * COLT, COLT), COLT)
        part[:, cols] = jnp.dot(comb_ref[...], rbuf[:, cols], preferred_element_type=jnp.float32)

    def of(block):
        return part[pl.ds(pl.multiple_of(lax.rem(block + 2 * NZ, NZ) * TOK, TOK), TOK), :]

    zr = [remote(rsend.at[i], rrecv.at[i], zr_send.at[i], zr_recv.at[i], up) for i in range(RIGHT)]
    zl = [remote(lsend.at[i], lrecv.at[i], zl_send.at[i], zl_recv.at[i], down) for i in range(LEFT)]
    for i in range(RIGHT):
        if i > 0:
            zr[i - 1].wait_recv()
        value = of(z + RIGHT - i)
        if i > 0:
            value = value + rrecv[i - 1].astype(jnp.float32)
        rsend[i] = value.astype(jnp.bfloat16)
        zr[i].start()
        if i < LEFT:
            if i > 0:
                zl[i - 1].wait_recv()
            value = of(z - LEFT + i)
            if i > 0:
                value = value + lrecv[i - 1].astype(jnp.float32)
            lsend[i] = value.astype(jnp.bfloat16)
            zl[i].start()
    zr[RIGHT - 1].wait_recv()
    zl[LEFT - 1].wait_recv()
    total = of(z) + rrecv[RIGHT - 1].astype(jnp.float32) + lrecv[LEFT - 1].astype(jnp.float32)
    out_ref[...] = total.astype(jnp.bfloat16)
    for copy in yr + yl + hr + hl + xcopies + zr + zl:
        copy.wait_send()


def experts(rows, gate, up, thr, dn, comb):
    vmem = pl.BlockSpec(memory_space=pltpu.VMEM)
    anyspace = pl.BlockSpec(memory_space=pl.ANY)
    dma = pltpu.SemaphoreType.DMA
    bf, f32 = jnp.bfloat16, jnp.float32
    return pl.pallas_call(
        expert_kernel,
        out_shape=jax.ShapeDtypeStruct((TOK, WIDTH), bf),
        in_specs=[anyspace, anyspace, anyspace, vmem, anyspace, vmem],
        out_specs=vmem,
        scratch_shapes=[
            pltpu.VMEM((NY, ROWS, WIDTH), bf),
            pltpu.VMEM((D, HID), bf),
            pltpu.VMEM((D, HID), bf),
            pltpu.VMEM((ROWS, HID), f32),
            pltpu.VMEM((ROWS, HID), f32),
            pltpu.VMEM((NY, ROWS, HID), bf),
            pltpu.VMEM((NY * HID, WIDTH), bf),
            pltpu.VMEM((ROWS, WIDTH), bf),
            pltpu.VMEM((ROWS, WIDTH), bf),
            pltpu.VMEM((STOK, WIDTH), f32),
            pltpu.VMEM((RIGHT, TOK, WIDTH), bf),
            pltpu.VMEM((RIGHT, TOK, WIDTH), bf),
            pltpu.VMEM((LEFT, TOK, WIDTH), bf),
            pltpu.VMEM((LEFT, TOK, WIDTH), bf),
            dma((3,)), dma((3,)), dma((3,)), dma((3,)),
            dma((3,)), dma((3,)), dma((3,)), dma((3,)),
            dma((NG - 1,)), dma((NG - 1,)),
            dma((RIGHT,)), dma((RIGHT,)), dma((LEFT,)), dma((LEFT,)),
            dma((5,)),
        ],
        compiler_params=pltpu.CompilerParams(
            collective_id=1, has_side_effects=True, vmem_limit_bytes=62 * 1024 * 1024
        ),
        name="experts",
    )(rows, gate, up, thr, dn, comb)


def on_device(tokens, expert_ids, route_weights, gate_weight, up_weight, down_weight):
    bf, f32 = jnp.bfloat16, jnp.float32
    experts_n = NG * NZ
    w_local = jnp.maximum(
        jnp.max(jnp.abs(gate_weight[0]), axis=1), jnp.max(jnp.abs(up_weight[0]), axis=1)
    ).reshape(WROWS, 128)

    named = expert_ids[:, :, None] == jnp.arange(experts_n, dtype=jnp.int32)
    chosen = jnp.any(named, axis=1).astype(bf)
    earlier = (np.arange(TOK)[:, None] > np.arange(TOK)[None, :]).astype(np.float32)
    before = jnp.dot(jnp.asarray(earlier, bf), chosen, preferred_element_type=f32)
    place_of = jnp.sum(jnp.where(named, before[:, None, :], 0.0), axis=2)
    meta = jnp.concatenate(
        [expert_ids.astype(bf), place_of.astype(bf), route_weights.astype(bf),
         jnp.zeros((TOK, 128 - 3 * TOP), bf)], axis=1)
    aux = jnp.concatenate([meta, w_local, jnp.zeros((AUX - TOK - WROWS, 128), bf)], axis=0)

    r = np.arange(ROWS)
    group, zz, p = r // PIECE, (r % PIECE) // CAP, r % CAP
    fixed = ((group // NC) * (NZ * NC) + group % NC) * CODE + p + 1024 * zz
    z = lax.rem(lax.axis_index("expert") // NC, NZ)
    key = jnp.asarray(fixed, f32) + (z * NC * CODE).astype(f32)
    keyrow = jnp.broadcast_to(key[None, :], (8, ROWS))
    keycol = jnp.broadcast_to(key[:, None], (ROWS, 128))

    rows, dn, comb, most = dispatch(tokens, aux, keyrow, keycol, down_weight[0])

    wt_max = jnp.max(most[:, :WROWS], axis=0).reshape(D)
    act_max = most[:, WROWS : WROWS + AROWS].reshape(D)
    scales = jnp.sqrt((act_max + EPS) / (wt_max + EPS))
    clip_limit = CLIP_SHARE * jnp.max(act_max / scales)
    thr = (clip_limit * scales).astype(bf).reshape(NY, 1, WIDTH)
    thr = jnp.broadcast_to(thr, (NY, 16, WIDTH)).reshape(NY * 16, WIDTH)
    out = experts(
        rows.reshape(ROWS, WIDTH), gate_weight[0], up_weight[0], thr, dn.reshape(NY * HID, WIDTH), comb
    )
    own_part = lax.dynamic_slice_in_dim(scales, lax.axis_index("tensor") * WIDTH, WIDTH)
    return (out, own_part)


def solution(mesh):
    placed = (
        P("expert", "tensor"),
        P("expert", None),
        P("expert", None),
        P("expert", None, "tensor"),
        P("expert", None, "tensor"),
        P("expert", "tensor", None),
    )
    return jax.shard_map(
        on_device,
        mesh=mesh,
        in_specs=placed,
        out_specs=(P("expert", "tensor"), P("tensor")),
        check_vma=False,
    )
```
